32 devices in a mesh: chan: 4 (over y, core), tile: 8 (over z, x).
Axes of the slice: x: 2, y: 2, z: 4, core: 2. Of those that a mesh axis runs over, the one named last changes fastest.
Arguments:
- dirty: float32 [2, 36, 128, 128], P(None, 'chan', 'tile'), may hold values from -6 to 6
- beams: float32 [36, 289], P('chan'), may hold values from -0.24 to 0.24
- chan_bins: int32 [36], replicated, may hold values from 0 to 287
- pixel_order: int32 [8, 2048], P('tile'), may hold values from 0 to 2047, each once within a row
Outputs:
- spectrum: float32 [2, 256, 8, 2048], P(None, None, 'tile', 'chan')
- residual: float32 [2, 36, 128, 128], P(None, 'chan', 'tile')
The draws below stay inside these ranges and needn't reach their ends.
Inputs may be any that keep to these rules, and one draw needn't show every extreme that they name: `pixel_order`: each row is a permutation of 0 to 2047.
All inputs are finite; a program needn't handle non-finite values.
Results may differ from the reference program's by a relative error of at most 0.000068.
Values sent between devices are 32-bit elements; how exact they have to be, the bound alone decides.
A program may use at most 64 MiB of HBM per device.

```python
import math
import jax
import jax.numpy as jnp
from jax import lax

CHANNELS = 36
DEPTHS = 256
BINS = 288
BEAM = 17
HALF = 8
NX = 128
NY = 128
TILES = 8
TILE_PIX = 2048


def with_ends(result, key, smallest, largest):
    spot = [jax.random.randint(jax.random.fold_in(key, axis), (), 0, length) for axis, length in enumerate(result.shape)]
    widest = result.shape.index(max(result.shape))
    next_to = spot[:widest] + [(spot[widest] + 1) % result.shape[widest]] + spot[widest + 1:]
    return result.at[tuple(spot)].set(smallest).at[tuple(next_to)].set(largest)


def block_levels(stream_key, dims, shards, low, high):
    loudness, own = 1.0, jax.random.fold_in(stream_key, 6)
    for dim, parts in shards:
        steps = jnp.exp(jax.random.uniform(jax.random.fold_in(own, dim), (parts,), jnp.float32, low / len(shards), high / len(shards)))
        loudness = loudness * jnp.repeat(steps, dims[dim] // parts).reshape([-1 if axis == dim else 1 for axis in range(len(dims))])
    return loudness


def centred(stream_key, extent, deviation, bound, cuts=(), kind=jnp.bfloat16):
    drawn = jax.random.normal(stream_key, extent, jnp.float32) * deviation
    if len(cuts) > 0:
        drawn = block_levels(stream_key, extent, cuts, -0.22, 0.18) * drawn
    return jnp.clip(drawn, min=-bound, max=bound).astype(kind)


def setup_inputs(seed: int = 0) -> dict:
    seeds = jax.random.split(jax.random.key(seed), 5)
    dirty = centred(seeds[0], (2, CHANNELS, NY, NX), 1.0, 6.0, ((1, 4), (2, 8)), jnp.float32)
    beams = centred(seeds[1], (CHANNELS, BEAM * BEAM), 0.04, 0.24, ((0, 4),), jnp.float32)
    chan_bins = with_ends(jax.random.randint(seeds[2], (CHANNELS,), 0, BINS), jax.random.fold_in(seeds[2], 1), 0, BINS - 1).astype(jnp.int32)
    pixel_order = jax.vmap(lambda own: jax.random.permutation(own, TILE_PIX))(jax.random.split(seeds[3], TILES)).reshape((TILES, TILE_PIX)).astype(jnp.int32)
    return {"dirty": dirty, "beams": beams, "chan_bins": chan_bins, "pixel_order": pixel_order}


THRESHOLD = 0.8
STEP_SIZE = 0.5
HIGH = lax.Precision.HIGHEST

def analysis_matrix(bin_list, channels):
    depth_index = jnp.arange(DEPTHS, dtype=jnp.int32) - DEPTHS // 2
    turn_count = jnp.mod(bin_list[:, None] * depth_index[None, :], BINS)
    angles = turn_count.astype(jnp.float32) * (2.0 * math.pi / BINS)
    cosine = jnp.cos(angles).T
    sine_part = jnp.sin(angles).T
    upper = jnp.concatenate([cosine, sine_part], axis=1)
    lower = jnp.concatenate([-sine_part, cosine], axis=1)
    return jnp.concatenate([upper, lower], axis=0) * (1.0 / math.sqrt(channels))

def shrink(spectra):
    depth_count = spectra.shape[0] // 2
    real_part = spectra[:depth_count]
    imag_part = spectra[depth_count:]
    magnitude = jnp.sqrt(real_part * real_part + imag_part * imag_part)
    factor = jnp.maximum(magnitude - THRESHOLD, 0.0) / jnp.maximum(magnitude, THRESHOLD)
    return spectra * jnp.concatenate([factor, factor], axis=0)

def blur(field, beams, row_pad):
    pair_count, chan_count, row_count, col_count = field.shape
    beam_width = math.isqrt(beams.shape[1])
    beam_edge = (beam_width - 1) // 2
    kernel = beams.reshape(chan_count, beam_width, beam_width)
    kernel = jnp.concatenate([kernel, kernel], axis=0)[:, None]
    stacked = field.reshape(1, pair_count * chan_count, row_count, col_count)
    blurred = lax.conv_general_dilated(stacked, kernel, (1, 1), ((row_pad, row_pad), (beam_edge, beam_edge)), feature_group_count=pair_count * chan_count, precision=HIGH)
    return blurred.reshape(pair_count, chan_count, blurred.shape[2], col_count)

def reference(dirty, beams, chan_bins, pixel_order):
    channels = chan_bins.shape[0]
    analysis = analysis_matrix(chan_bins, channels)
    observed = dirty.reshape(2 * channels, NY * NX)
    first = shrink(jnp.dot(analysis, observed, precision=HIGH, preferred_element_type=jnp.float32))
    model = jnp.dot(analysis.T, first, precision=HIGH, preferred_element_type=jnp.float32)
    model = model.reshape(2, channels, NY, NX)
    residual = dirty - blur(model, beams, HALF)
    update = jnp.dot(analysis, residual.reshape(2 * channels, NY * NX), precision=HIGH, preferred_element_type=jnp.float32)
    second = shrink(first + STEP_SIZE * update)
    arranged = second.reshape(2 * DEPTHS, TILES, TILE_PIX)
    slot_index = jnp.broadcast_to(pixel_order[None], arranged.shape)
    spectrum = jnp.take_along_axis(arranged, slot_index, axis=2).reshape(2, DEPTHS, TILES, TILE_PIX)
    return (spectrum, residual)
```

```python
import functools
import math

import jax
import jax.numpy as jnp
from jax import lax
from jax.experimental import pallas as pl
from jax.experimental.pallas import tpu as pltpu
from jax.sharding import PartitionSpec as P

DEPTHS = 256
BINS = 288
THRESHOLD = 0.8
STEP_SIZE = 0.5
MESH = pl.DeviceIdType.MESH
LANES = 128
F32 = jnp.float32
BF16 = jnp.bfloat16


def round_up(value, unit):
    return (value + unit - 1) // unit * unit


def split(x):
    high = x.astype(BF16)
    return high, (x - high.astype(F32)).astype(BF16)


def shrink_pair(a, b):
    squared = a * a + b * b
    factor = jnp.maximum(1.0 - THRESHOLD * lax.rsqrt(jnp.maximum(squared, 1e-30)), 0.0)
    return a * factor, b * factor


def mxu(a, b):
    return jnp.dot(a, b, preferred_element_type=F32)


def kernel(
    d,
    dirty,
    beams,
    bins,
    order,
    out,
    res,
    bincol,
    at3,
    a3,
    at2,
    x,
    big,
    first_hi,
    first_lo,
    first_slots,
    model,
    padded,
    slots,
    mixed,
    send_a,
    send_d,
    send_m,
    send_r,
    recv_a,
    recv_d,
    recv_m,
    recv_h,
    recv_r,
    sems_a,
    sems_d,
    sems_m,
    sems_h,
    sems_r,
):
    G, T, R, Y, C, S, W, CC, NCH, HALF, BEAM = (
        d["G"], d["T"], d["R"], d["Y"], d["C"], d["S"], d["W"], d["CC"], d["NCH"], d["HALF"], d["BEAM"]
    )
    SC = S * C
    KP = d["KP"]
    g = lax.axis_index("chan")
    t = lax.axis_index("tile")
    has_prev = t > 0
    has_next = t < T - 1
    before = lax.rem(t + T - 1, T)
    after = lax.rem(t + 1, T)

    barrier = pltpu.get_barrier_semaphore()
    for step in range(1, G):
        pl.semaphore_signal(barrier, inc=1, device_id=(lax.rem(g + step, G), t), device_id_type=MESH)

    @pl.when(has_prev)
    def _():
        for p in range(G):
            pl.semaphore_signal(barrier, inc=1, device_id=(p, before), device_id_type=MESH)

    @pl.when(has_next)
    def _():
        for p in range(G):
            pl.semaphore_signal(barrier, inc=1, device_id=(p, after), device_id_type=MESH)

    def pack(send, k, cells):
        for p in range(G):
            for r in range(R):
                send[p, k, r * W : r * W + W, :] = cells[pl.ds(k * W * Y + p * R + r, W, stride=Y), :]

    for c in range(C):
        for s in range(S):
            mixed[(c * S + s) * Y : (c * S + s) * Y + Y, :] = dirty[(s * C + c) * Y : (s * C + c) * Y + Y, :]
    for k in range(NCH):
        pack(send_a, k, mixed)
    near = has_prev.astype(jnp.int32) + has_next.astype(jnp.int32)
    pl.semaphore_wait(barrier, G - 1 + G * near)

    def own_copies(src, dst, sems, *k):
        out_copies, in_copies = [], []
        for step in range(1, G):
            p = lax.rem(g + step, G)
            out_copies.append(
                pltpu.make_async_remote_copy(
                    src(p), dst(g), sems.at[(0, p, *k)], sems.at[(1, g, *k)], device_id=(p, t), device_id_type=MESH
                )
            )
            in_copies.append(
                pltpu.make_async_remote_copy(
                    src(p), dst(p), sems.at[(0, p, *k)], sems.at[(1, p, *k)], device_id=(p, t), device_id_type=MESH
                )
            )
        return out_copies, in_copies

    out_a, in_a = own_copies(lambda p: send_a.at[p], lambda p: recv_a.at[p], sems_a)
    for copy in out_a:
        copy.start()
    recv_a[g] = send_a[g]

    bincol[...] = jnp.zeros_like(bincol)
    for row in range(G * C):
        bincol[S * row : S * row + S, :] = jnp.full((S, LANES), bins[row].astype(F32))
    scale = 1.0 / math.sqrt(G * C)
    at3[...] = jnp.zeros_like(at3)
    for piece in range(DEPTHS // LANES):
        shape = (KP, LANES)
        depth = lax.broadcasted_iota(jnp.int32, shape, 1) + (piece * LANES - DEPTHS // 2)
        product = bincol[...] * depth.astype(F32)
        turns = product - BINS * jnp.floor(product * (1.0 / BINS))
        turns = jnp.where(turns < 0, turns + BINS, turns)
        turns = jnp.where(turns >= BINS, turns - BINS, turns)
        angles = turns * (2.0 * math.pi / BINS)
        row = lax.broadcasted_iota(jnp.int32, shape, 0)
        is_q = (row & 1) == 0
        real = row < G * SC
        cosine = jnp.where(real, jnp.cos(angles) * scale, 0.0)
        sine = jnp.where(real, jnp.sin(angles) * scale, 0.0)
        for half, value in ((0, jnp.where(is_q, cosine, sine)), (1, jnp.where(is_q, -sine, cosine))):
            lanes = pl.ds(half * DEPTHS + piece * LANES, LANES)
            high, low = split(value)
            at2[0:KP, lanes] = high
            at2[KP : 2 * KP, lanes] = low
            at3[0:KP, lanes] = high.astype(F32)
            at3[KP : 2 * KP, lanes] = low.astype(F32)
            at3[2 * KP : 3 * KP, lanes] = high.astype(F32)
    a3[...] = at3[...].T.astype(BF16)
    x[...] = jnp.zeros_like(x)

    shift = int(math.log2(LANES))

    def permute(cells):
        halves = []
        for h in range(Y // 8):
            pixel = order[8 * h : 8 * h + 8, :]
            col = pixel & (LANES - 1)
            row = lax.shift_right_logical(pixel, shift)
            acc = jnp.zeros((8, LANES), F32)
            for y in range(Y):
                taken = jnp.take_along_axis(cells(y), col, axis=1, mode="promise_in_bounds")
                acc = jnp.where(row == y, taken, acc)
            halves.append(acc)
        return jnp.concatenate(halves, axis=0)

    def gather_dirty(c, carry):
        for s in range(S):
            source = (s * C + c) * Y
            target = pl.ds(pl.multiple_of((c * S + s) * Y, 8), Y)
            slots[target, :] = permute(lambda y: jnp.broadcast_to(dirty[pl.ds(source + y, 1), :], (8, LANES)))
        return carry

    lax.fori_loop(0, C, gather_dirty, 0)
    for k in range(NCH):
        pack(send_d, k, slots)
    out_d, in_d = own_copies(lambda p: send_d.at[p], lambda p: recv_d.at[p], sems_d)
    for copy in out_d:
        copy.start()
    recv_d[g] = send_d[g]

    def project(recv):
        for q in range(G):
            for k in range(NCH):
                for r in range(R):
                    x[q * SC + k * W : q * SC + k * W + W, r * LANES : (r + 1) * LANES] = recv[
                        q, k, r * W : r * W + W, :
                    ]
        high, low = split(x[...])
        parts = [high, high, low]
        if d["K3"] > 3 * KP:
            parts.append(jnp.zeros((d["K3"] - 3 * KP, x.shape[1]), BF16))
        big[...] = mxu(a3[...], jnp.concatenate(parts, axis=0))

    BLOCK = 16

    for copy in in_a:
        copy.wait_recv()
    project(recv_a)

    def shrink_first(i, carry):
        top = pl.ds(pl.multiple_of(i * BLOCK, BLOCK), BLOCK)
        low = pl.ds(pl.multiple_of(DEPTHS + i * BLOCK, BLOCK), BLOCK)
        a, b = shrink_pair(big[top, :], big[low, :])
        first_hi[top, :], first_lo[top, :] = split(a)
        first_hi[low, :], first_lo[low, :] = split(b)
        return carry

    lax.fori_loop(0, DEPTHS // BLOCK, shrink_first, 0)
    both = mxu(at2[...], first_hi[...])
    model[...] = both[:KP] + both[KP:] + mxu(at2[0:KP, :], first_lo[...])

    up = g * R < HALF
    goes = jnp.logical_or(jnp.logical_and(up, has_prev), jnp.logical_and(jnp.logical_not(up), has_next))
    toward = jnp.where(up, before, after)
    copies_m, copies_h = [], []
    for k in range(NCH):
        for p in range(G):
            for r in range(R):
                send_m[p, k, r * W : r * W + W, :] = model[
                    p * SC + k * W : p * SC + k * W + W, r * LANES : (r + 1) * LANES
                ]
        halo = [
            pltpu.make_async_remote_copy(
                send_m.at[p, k],
                recv_h.at[g, k],
                sems_h.at[0, p, k],
                sems_h.at[1, g, k],
                device_id=(p, toward),
                device_id_type=MESH,
            )
            for p in range(G)
        ]
        copies_h.append(halo)

        @pl.when(goes)
        def _():
            for copy in halo:
                copy.start()

        copies = own_copies(
            lambda p: send_m.at[p, k], lambda p: recv_m.at[p, k], sems_m, k
        )
        copies_m.append(copies)
        for copy in copies[0]:
            copy.start()
        recv_m[g, k] = send_m[g, k]

    for copy in in_d:
        copy.wait_recv()
    project(recv_d)

    def shrink_slots(i, carry):
        top = pl.ds(pl.multiple_of(i * BLOCK, BLOCK), BLOCK)
        low = pl.ds(pl.multiple_of(DEPTHS + i * BLOCK, BLOCK), BLOCK)
        first_slots[top, :], first_slots[low, :] = shrink_pair(big[top, :], big[low, :])
        return carry

    lax.fori_loop(0, DEPTHS // BLOCK, shrink_slots, 0)

    PY = Y + 2 * HALF
    lane = lax.broadcasted_iota(jnp.int32, (Y, LANES), 1)
    blocks = [range(0, (BEAM + 1) // 2), range((BEAM + 1) // 2, BEAM)]

    def convolve(c, carry):
        totals = [jnp.zeros((Y, LANES), F32) for _ in range(S)]
        for block in blocks:
            sums = [[None] * len(block) for _ in range(S)]
            for i in range(BEAM):
                rows = [padded[pl.ds((c * S + s) * PY + i, Y), :] for s in range(S)]
                for n, j in enumerate(block):
                    tap = beams[c, i * BEAM + j]
                    for s in range(S):
                        term = tap * rows[s]
                        sums[s][n] = term if i == 0 else sums[s][n] + term
            for n, j in enumerate(block):
                inside = jnp.logical_and(lane + (j - HALF) >= 0, lane + (j - HALF) < LANES)
                for s in range(S):
                    moved = sums[s][n]
                    if j != HALF:
                        moved = pltpu.roll(moved, (HALF - j) % LANES, axis=1)
                        moved = jnp.where(inside, moved, 0.0)
                    totals[s] = totals[s] + moved
        for s in range(S):
            cells = pl.ds(pl.multiple_of((s * C + c) * Y, 8), Y)
            res[cells, :] = dirty[cells, :] - totals[s]
        return carry

    def gather_res(c, carry):
        for s in range(S):
            source = (s * C + c) * Y
            target = pl.ds(pl.multiple_of((c * S + s) * Y, 8), Y)
            slots[target, :] = permute(lambda y: jnp.broadcast_to(res[pl.ds(source + y, 1), :], (8, LANES)))
        return carry

    def halo_block(q, k, ok):
        arrived = pltpu.make_async_remote_copy(
            send_m.at[q, k],
            recv_h.at[q, k],
            sems_h.at[0, q, k],
            sems_h.at[1, q, k],
            device_id=(q, t),
            device_id_type=MESH,
        )

        @pl.when(ok)
        def _():
            arrived.wait_recv()

        @pl.when(jnp.logical_not(ok))
        def _():
            recv_h[q, k] = jnp.zeros(recv_h.shape[2:], F32)

    copies_r = []
    for k in range(NCH):
        for copy in copies_m[k][1]:
            copy.wait_recv()
        for q in range(G):
            from_next = q * R < HALF
            halo_block(q, k, has_next if from_next else has_prev)
            at_row = Y + HALF + q * R if from_next else q * R - HALF
            for r in range(R):
                padded[pl.ds(k * W * PY + HALF + q * R + r, W, stride=PY), :] = recv_m[
                    q, k, r * W : r * W + W, :
                ]
                padded[pl.ds(k * W * PY + at_row + r, W, stride=PY), :] = recv_h[
                    q, k, r * W : r * W + W, :
                ]
        lax.fori_loop(k * CC, (k + 1) * CC, convolve, 0)
        lax.fori_loop(k * CC, (k + 1) * CC, gather_res, 0)
        pack(send_r, k, slots)
        copies = own_copies(
            lambda p: send_r.at[p, k], lambda p: recv_r.at[p, k], sems_r, k
        )
        copies_r.append(copies)
        for copy in copies[0]:
            copy.start()
        recv_r[g, k] = send_r[g, k]

    for k in range(NCH):
        for copy in copies_r[k][1]:
            copy.wait_recv()
    project(recv_r)

    def finish(i, carry, tail=0):
        top = pl.ds(pl.multiple_of(i * BLOCK, BLOCK), BLOCK)
        low = pl.ds(pl.multiple_of(DEPTHS + i * BLOCK, BLOCK), BLOCK)
        a, b = shrink_pair(
            first_slots[top, :] + STEP_SIZE * big[top, :], first_slots[low, :] + STEP_SIZE * big[low, :]
        )
        for start, value in ((0, a), (DEPTHS, b)):
            for r in range(R):
                piece = value[:, r * LANES : (r + 1) * LANES]
                base = (start + i * BLOCK) * R + r
                out[pl.ds(base, BLOCK - tail, stride=R), :] = piece[: BLOCK - tail]
                if tail:
                    out[pl.ds(base + (BLOCK - tail) * R, tail), :] = piece[BLOCK - tail :]
        return carry

    lax.fori_loop(0, DEPTHS // BLOCK - 1, finish, 0)
    finish(DEPTHS // BLOCK - 1, 0, 1)

    for copy in out_a + out_d:
        copy.wait_send()
    for k in range(NCH):
        for copy in copies_m[k][0] + copies_r[k][0]:
            copy.wait_send()

    @pl.when(goes)
    def _():
        for halo in copies_h:
            for copy in halo:
                copy.wait_send()


def on_device(dirty, beams, chan_bins, pixel_order):
    S, C, Y, X = dirty.shape
    G = lax.axis_size("chan")
    T = lax.axis_size("tile")
    BEAM = math.isqrt(beams.shape[1])
    HALF = (BEAM - 1) // 2
    R = Y // G
    CC = 3 if C % 3 == 0 else C
    NCH = C // CC
    W = S * CC
    SC = S * C
    KP = round_up(G * SC, 16)
    K3 = round_up(3 * KP, LANES)
    PB = round_up(R * W, 8)
    N = R * X
    d = dict(G=G, T=T, R=R, Y=Y, C=C, S=S, W=W, CC=CC, NCH=NCH, HALF=HALF, BEAM=BEAM, KP=KP, K3=K3)
    vmem = pl.BlockSpec(memory_space=pltpu.VMEM)
    smem = pl.BlockSpec(memory_space=pltpu.SMEM)
    block = pltpu.VMEM((G, NCH, PB, LANES), F32)
    dma = pltpu.SemaphoreType.DMA
    spectrum, residual = pl.pallas_call(
        functools.partial(kernel, d),
        out_shape=(
            jax.ShapeDtypeStruct((2 * DEPTHS * R, LANES), F32),
            jax.ShapeDtypeStruct((SC * Y, X), F32),
        ),
        in_specs=[vmem, smem, smem, vmem],
        out_specs=(vmem, vmem),
        scratch_shapes=[
            pltpu.VMEM((KP, LANES), F32),
            pltpu.VMEM((K3, 2 * DEPTHS), F32),
            pltpu.VMEM((2 * DEPTHS, K3), BF16),
            pltpu.VMEM((2 * KP, 2 * DEPTHS), BF16),
            pltpu.VMEM((KP, N), F32),
            pltpu.VMEM((2 * DEPTHS, N), F32),
            pltpu.VMEM((2 * DEPTHS, N), BF16),
            pltpu.VMEM((2 * DEPTHS, N), BF16),
            pltpu.VMEM((2 * DEPTHS, N), F32),
            pltpu.VMEM((KP, N), F32),
            pltpu.VMEM(((SC + 1) * (Y + 2 * HALF), LANES), F32),
            pltpu.VMEM(((SC + 1) * Y, LANES), F32),
            pltpu.VMEM(((SC + 1) * Y, LANES), F32),
        ]
        + [block] * 9
        + [dma((2, G)), dma((2, G)), dma((2, G, NCH)), dma((2, G, NCH)), dma((2, G, NCH))],
        compiler_params=pltpu.CompilerParams(
            collective_id=0, has_side_effects=True, vmem_limit_bytes=48 * 1024 * 1024
        ),
    )(dirty.reshape(SC * Y, X), beams, chan_bins, pixel_order.reshape(Y, X))
    return spectrum.reshape(2, DEPTHS, 1, N), residual.reshape(dirty.shape)


def solution(mesh):
    placed = (P(None, "chan", "tile", None), P("chan", None), P(), P("tile", None))
    return jax.shard_map(
        on_device,
        mesh=mesh,
        in_specs=placed,
        out_specs=(P(None, None, "tile", "chan"), P(None, "chan", "tile", None)),
        check_vma=False,
    )
```

```python
import functools
import math

import jax
import jax.numpy as jnp
from jax import lax
from jax.experimental import pallas as pl
from jax.experimental.pallas import tpu as pltpu
from jax.sharding import PartitionSpec as P

DEPTHS = 256
BINS = 288
THRESHOLD = 0.8
STEP_SIZE = 0.5
MESH = pl.DeviceIdType.MESH
LANES = 128
F32 = jnp.float32
BF16 = jnp.bfloat16


def round_up(value, unit):
    return (value + unit - 1) // unit * unit


def split(x):
    high = x.astype(BF16)
    return high, (x - high.astype(F32)).astype(BF16)


def shrink_pair(a, b):
    squared = a * a + b * b
    factor = jnp.maximum(1.0 - THRESHOLD * lax.rsqrt(jnp.maximum(squared, 1e-30)), 0.0)
    return a * factor, b * factor


def aligned(row):
    return row if isinstance(row, int) else pl.multiple_of(row, 8)


def mxu(a, b):
    return jnp.dot(a, b, preferred_element_type=F32)


def kernel(
    d,
    dirty_hbm,
    beams_hbm,
    bins_hbm,
    order_hbm,
    out,
    res,
    dirty,
    beams,
    bins,
    order,
    bincol,
    at3,
    a3,
    at2,
    x,
    big,
    first_hi,
    first_lo,
    first_slots,
    model,
    padded,
    slots,
    mixed,
    send_a,
    send_d,
    send_m,
    send_r,
    recv_a,
    recv_d,
    recv_m,
    recv_h,
    recv_r,
    sems_a,
    sems_d,
    sems_m,
    sems_h,
    sems_r,
    sems_in,
):
    G, T, R, Y, C, S, W, CC, NCH, HALF, BEAM = (
        d["G"], d["T"], d["R"], d["Y"], d["C"], d["S"], d["W"], d["CC"], d["NCH"], d["HALF"], d["BEAM"]
    )
    SC = S * C
    KP = d["KP"]
    g = lax.axis_index("chan")
    t = lax.axis_index("tile")
    has_prev = t > 0
    has_next = t < T - 1
    before = lax.rem(t + T - 1, T)
    after = lax.rem(t + 1, T)

    pairs = ((dirty_hbm, dirty), (bins_hbm, bins), (beams_hbm, beams), (order_hbm, order))
    loads = [pltpu.make_async_copy(src, dst, sems_in.at[n]) for n, (src, dst) in enumerate(pairs)]
    for load in loads:
        load.start()
    barrier = pltpu.get_barrier_semaphore()
    for step in range(1, G):
        pl.semaphore_signal(barrier, inc=1, device_id=(lax.rem(g + step, G), t), device_id_type=MESH)

    @pl.when(has_prev)
    def _():
        for p in range(G):
            pl.semaphore_signal(barrier, inc=1, device_id=(p, before), device_id_type=MESH)

    @pl.when(has_next)
    def _():
        for p in range(G):
            pl.semaphore_signal(barrier, inc=1, device_id=(p, after), device_id_type=MESH)

    def pack(send, k, cells):
        for p in range(G):
            for r in range(R):
                send[p, k, r * W : r * W + W, :] = cells[pl.ds(k * W * Y + p * R + r, W, stride=Y), :]

    loads[0].wait()
    for c in range(C):
        for s in range(S):
            mixed[(c * S + s) * Y : (c * S + s) * Y + Y, :] = dirty[(s * C + c) * Y : (s * C + c) * Y + Y, :]
    for k in range(NCH):
        pack(send_a, k, mixed)
    near = has_prev.astype(jnp.int32) + has_next.astype(jnp.int32)
    pl.semaphore_wait(barrier, G - 1 + G * near)

    def own_copies(src, dst, sems, *k):
        out_copies, in_copies = [], []
        for step in range(1, G):
            p = lax.rem(g + step, G)
            out_copies.append(
                pltpu.make_async_remote_copy(
                    src(p), dst(g), sems.at[(0, p, *k)], sems.at[(1, g, *k)], device_id=(p, t), device_id_type=MESH
                )
            )
            in_copies.append(
                pltpu.make_async_remote_copy(
                    src(p), dst(p), sems.at[(0, p, *k)], sems.at[(1, p, *k)], device_id=(p, t), device_id_type=MESH
                )
            )
        return out_copies, in_copies

    out_a, in_a = own_copies(lambda p: send_a.at[p], lambda p: recv_a.at[p], sems_a)
    for copy in out_a:
        copy.start()
    recv_a[g] = send_a[g]

    for load in loads[1:]:
        load.wait()
    bincol[...] = jnp.zeros_like(bincol)
    for row in range(G * C):
        bincol[S * row : S * row + S, :] = jnp.full((S, LANES), bins[row].astype(F32))
    scale = 1.0 / math.sqrt(G * C)
    at3[...] = jnp.zeros_like(at3)
    for piece in range(DEPTHS // LANES):
        shape = (KP, LANES)
        depth = lax.broadcasted_iota(jnp.int32, shape, 1) + (piece * LANES - DEPTHS // 2)
        product = bincol[...] * depth.astype(F32)
        turns = product - BINS * jnp.floor(product * (1.0 / BINS))
        turns = jnp.where(turns < 0, turns + BINS, turns)
        turns = jnp.where(turns >= BINS, turns - BINS, turns)
        angles = turns * (2.0 * math.pi / BINS)
        row = lax.broadcasted_iota(jnp.int32, shape, 0)
        is_q = (row & 1) == 0
        real = row < G * SC
        cosine = jnp.where(real, jnp.cos(angles) * scale, 0.0)
        sine = jnp.where(real, jnp.sin(angles) * scale, 0.0)
        for half, value in ((0, jnp.where(is_q, cosine, sine)), (1, jnp.where(is_q, -sine, cosine))):
            lanes = pl.ds(half * DEPTHS + piece * LANES, LANES)
            high, low = split(value)
            at2[0:KP, lanes] = high
            at2[KP : 2 * KP, lanes] = low
            at3[0:KP, lanes] = high.astype(F32)
            at3[KP : 2 * KP, lanes] = low.astype(F32)
            at3[2 * KP : 3 * KP, lanes] = high.astype(F32)
    a3[...] = at3[...].T.astype(BF16)
    x[...] = jnp.zeros_like(x)

    shift = int(math.log2(LANES))

    def permute(cells):
        halves = []
        for h in range(Y // 8):
            pixel = order[8 * h : 8 * h + 8, :]
            col = pixel & (LANES - 1)
            row = lax.shift_right_logical(pixel, shift)
            acc = jnp.zeros((8, LANES), F32)
            for y in range(Y):
                taken = jnp.take_along_axis(cells(y), col, axis=1, mode="promise_in_bounds")
                acc = jnp.where(row == y, taken, acc)
            halves.append(acc)
        return jnp.concatenate(halves, axis=0)

    def gather_dirty(c, carry):
        for s in range(S):
            source = (s * C + c) * Y
            target = pl.ds(aligned((c * S + s) * Y), Y)
            slots[target, :] = permute(lambda y: jnp.broadcast_to(dirty[pl.ds(source + y, 1), :], (8, LANES)))
        return carry

    def project(recv):
        for q in range(G):
            for k in range(NCH):
                for r in range(R):
                    x[q * SC + k * W : q * SC + k * W + W, r * LANES : (r + 1) * LANES] = recv[
                        q, k, r * W : r * W + W, :
                    ]
        high, low = split(x[...])
        parts = [high, high, low]
        if d["K3"] > 3 * KP:
            parts.append(jnp.zeros((d["K3"] - 3 * KP, x.shape[1]), BF16))
        big[...] = mxu(a3[...], jnp.concatenate(parts, axis=0))

    BLOCK = 16

    for copy in in_a:
        copy.wait_recv()
    project(recv_a)

    def shrink_first(i, carry):
        top = pl.ds(pl.multiple_of(i * BLOCK, BLOCK), BLOCK)
        low = pl.ds(pl.multiple_of(DEPTHS + i * BLOCK, BLOCK), BLOCK)
        a, b = shrink_pair(big[top, :], big[low, :])
        first_hi[top, :], first_lo[top, :] = split(a)
        first_hi[low, :], first_lo[low, :] = split(b)
        return carry

    lax.fori_loop(0, DEPTHS // BLOCK, shrink_first, 0)
    both = mxu(at2[...], first_hi[...])
    model[...] = both[:KP] + both[KP:] + mxu(at2[0:KP, :], first_lo[...])

    up = g * R < HALF
    goes = jnp.logical_or(jnp.logical_and(up, has_prev), jnp.logical_and(jnp.logical_not(up), has_next))
    toward = jnp.where(up, before, after)
    copies_m, copies_h = [], []
    for k in range(NCH):
        for p in range(G):
            for r in range(R):
                send_m[p, k, r * W : r * W + W, :] = model[
                    p * SC + k * W : p * SC + k * W + W, r * LANES : (r + 1) * LANES
                ]
        halo = [
            pltpu.make_async_remote_copy(
                send_m.at[p, k],
                recv_h.at[g, k],
                sems_h.at[0, p, k],
                sems_h.at[1, g, k],
                device_id=(p, toward),
                device_id_type=MESH,
            )
            for p in range(G)
        ]
        copies_h.append(halo)

        @pl.when(goes)
        def _():
            for copy in halo:
                copy.start()

        copies = own_copies(
            lambda p: send_m.at[p, k], lambda p: recv_m.at[p, k], sems_m, k
        )
        copies_m.append(copies)
        for copy in copies[0]:
            copy.start()
        recv_m[g, k] = send_m[g, k]

    lax.fori_loop(0, C, gather_dirty, 0)
    for k in range(NCH):
        pack(send_d, k, slots)
    out_d, in_d = own_copies(lambda p: send_d.at[p], lambda p: recv_d.at[p], sems_d)
    for copy in out_d:
        copy.start()
    recv_d[g] = send_d[g]

    PY = Y + 2 * HALF
    lane = lax.broadcasted_iota(jnp.int32, (Y, LANES), 1)
    blocks = [range(0, (BEAM + 1) // 2), range((BEAM + 1) // 2, BEAM)]

    def convolve(c, carry):
        totals = [jnp.zeros((Y, LANES), F32) for _ in range(S)]
        for block in blocks:
            sums = [[None] * len(block) for _ in range(S)]
            for i in range(BEAM):
                rows = [padded[pl.ds((c * S + s) * PY + i, Y), :] for s in range(S)]
                for n, j in enumerate(block):
                    tap = beams[c, i * BEAM + j]
                    for s in range(S):
                        term = tap * rows[s]
                        sums[s][n] = term if i == 0 else sums[s][n] + term
            for n, j in enumerate(block):
                inside = jnp.logical_and(lane + (j - HALF) >= 0, lane + (j - HALF) < LANES)
                for s in range(S):
                    moved = sums[s][n]
                    if j != HALF:
                        moved = pltpu.roll(moved, (HALF - j) % LANES, axis=1)
                        moved = jnp.where(inside, moved, 0.0)
                    totals[s] = totals[s] + moved
        for s in range(S):
            cells = pl.ds(aligned((s * C + c) * Y), Y)
            res[cells, :] = dirty[cells, :] - totals[s]
        return carry

    def gather_res(c, carry):
        for s in range(S):
            source = (s * C + c) * Y
            target = pl.ds(aligned((c * S + s) * Y), Y)
            slots[target, :] = permute(lambda y: jnp.broadcast_to(res[pl.ds(source + y, 1), :], (8, LANES)))
        return carry

    def halo_block(q, k, ok):
        arrived = pltpu.make_async_remote_copy(
            send_m.at[q, k],
            recv_h.at[q, k],
            sems_h.at[0, q, k],
            sems_h.at[1, q, k],
            device_id=(q, t),
            device_id_type=MESH,
        )

        @pl.when(ok)
        def _():
            arrived.wait_recv()

        @pl.when(jnp.logical_not(ok))
        def _():
            recv_h[q, k] = jnp.zeros(recv_h.shape[2:], F32)

    copies_r = []

    def step(c, carry):
        gather_res(c - 1, 0)
        return convolve(c, carry)

    def send_slots(k):
        pack(send_r, k, slots)
        copies = own_copies(lambda p: send_r.at[p, k], lambda p: recv_r.at[p, k], sems_r, k)
        copies_r.append(copies)
        for copy in copies[0]:
            copy.start()
        recv_r[g, k] = send_r[g, k]

    for k in range(NCH):
        for copy in copies_m[k][1]:
            copy.wait_recv()
        for q in range(G):
            from_next = q * R < HALF
            halo_block(q, k, has_next if from_next else has_prev)
            at_row = Y + HALF + q * R if from_next else q * R - HALF
            for r in range(R):
                padded[pl.ds(k * W * PY + HALF + q * R + r, W, stride=PY), :] = recv_m[
                    q, k, r * W : r * W + W, :
                ]
                padded[pl.ds(k * W * PY + at_row + r, W, stride=PY), :] = recv_h[
                    q, k, r * W : r * W + W, :
                ]
        if k == 0:
            convolve(0, 0)
        else:
            step(k * CC, 0)
            send_slots(k - 1)
        lax.fori_loop(k * CC + 1, (k + 1) * CC, step, 0)
    gather_res(C - 1, 0)
    send_slots(NCH - 1)

    for copy in in_d:
        copy.wait_recv()
    project(recv_d)

    def shrink_slots(i, carry):
        top = pl.ds(pl.multiple_of(i * BLOCK, BLOCK), BLOCK)
        low = pl.ds(pl.multiple_of(DEPTHS + i * BLOCK, BLOCK), BLOCK)
        first_slots[top, :], first_slots[low, :] = shrink_pair(big[top, :], big[low, :])
        return carry

    lax.fori_loop(0, DEPTHS // BLOCK, shrink_slots, 0)

    for k in range(NCH):
        for copy in copies_r[k][1]:
            copy.wait_recv()
    project(recv_r)

    def finish(i, carry, tail=0):
        top = pl.ds(pl.multiple_of(i * BLOCK, BLOCK), BLOCK)
        low = pl.ds(pl.multiple_of(DEPTHS + i * BLOCK, BLOCK), BLOCK)
        a, b = shrink_pair(
            first_slots[top, :] + STEP_SIZE * big[top, :], first_slots[low, :] + STEP_SIZE * big[low, :]
        )
        for start, value in ((0, a), (DEPTHS, b)):
            for r in range(R):
                piece = value[:, r * LANES : (r + 1) * LANES]
                base = (start + i * BLOCK) * R + r
                out[pl.ds(base, BLOCK - tail, stride=R), :] = piece[: BLOCK - tail]
                if tail:
                    out[pl.ds(base + (BLOCK - tail) * R, tail), :] = piece[BLOCK - tail :]
        return carry

    lax.fori_loop(0, DEPTHS // BLOCK - 1, finish, 0)
    finish(DEPTHS // BLOCK - 1, 0, 1)

    for copy in out_a + out_d:
        copy.wait_send()
    for k in range(NCH):
        for copy in copies_m[k][0] + copies_r[k][0]:
            copy.wait_send()

    @pl.when(goes)
    def _():
        for halo in copies_h:
            for copy in halo:
                copy.wait_send()


def on_device(dirty, beams, chan_bins, pixel_order):
    S, C, Y, X = dirty.shape
    G = lax.axis_size("chan")
    T = lax.axis_size("tile")
    BEAM = math.isqrt(beams.shape[1])
    HALF = (BEAM - 1) // 2
    R = Y // G
    CC = 3 if C % 3 == 0 else C
    NCH = C // CC
    W = S * CC
    SC = S * C
    KP = round_up(G * SC, 16)
    K3 = round_up(3 * KP, LANES)
    PB = round_up(R * W, 8)
    N = R * X
    d = dict(G=G, T=T, R=R, Y=Y, C=C, S=S, W=W, CC=CC, NCH=NCH, HALF=HALF, BEAM=BEAM, KP=KP, K3=K3)
    vmem = pl.BlockSpec(memory_space=pltpu.VMEM)
    hbm = pl.BlockSpec(memory_space=pltpu.HBM)
    block = pltpu.VMEM((G, NCH, PB, LANES), F32)
    dma = pltpu.SemaphoreType.DMA
    spectrum, residual = pl.pallas_call(
        functools.partial(kernel, d),
        out_shape=(
            jax.ShapeDtypeStruct((2 * DEPTHS * R, LANES), F32),
            jax.ShapeDtypeStruct((SC * Y, X), F32),
        ),
        in_specs=[hbm, hbm, hbm, hbm],
        out_specs=(vmem, vmem),
        scratch_shapes=[
            pltpu.VMEM((SC * Y, X), F32),
            pltpu.SMEM(beams.shape, F32),
            pltpu.SMEM(chan_bins.shape, jnp.int32),
            pltpu.VMEM((Y, X), jnp.int32),
            pltpu.VMEM((KP, LANES), F32),
            pltpu.VMEM((K3, 2 * DEPTHS), F32),
            pltpu.VMEM((2 * DEPTHS, K3), BF16),
            pltpu.VMEM((2 * KP, 2 * DEPTHS), BF16),
            pltpu.VMEM((KP, N), F32),
            pltpu.VMEM((2 * DEPTHS, N), F32),
            pltpu.VMEM((2 * DEPTHS, N), BF16),
            pltpu.VMEM((2 * DEPTHS, N), BF16),
            pltpu.VMEM((2 * DEPTHS, N), F32),
            pltpu.VMEM((KP, N), F32),
            pltpu.VMEM(((SC + 1) * (Y + 2 * HALF), LANES), F32),
            pltpu.VMEM(((SC + 1) * Y, LANES), F32),
            pltpu.VMEM(((SC + 1) * Y, LANES), F32),
        ]
        + [block] * 9
        + [dma((2, G)), dma((2, G)), dma((2, G, NCH)), dma((2, G, NCH)), dma((2, G, NCH)), dma((4,))],
        compiler_params=pltpu.CompilerParams(
            collective_id=0, has_side_effects=True, vmem_limit_bytes=48 * 1024 * 1024
        ),
    )(dirty.reshape(SC * Y, X), beams, chan_bins, pixel_order.reshape(Y, X))
    return spectrum.reshape(2, DEPTHS, 1, N), residual.reshape(dirty.shape)


def solution(mesh):
    placed = (P(None, "chan", "tile", None), P("chan", None), P(), P("tile", None))
    return jax.shard_map(
        on_device,
        mesh=mesh,
        in_specs=placed,
        out_specs=(P(None, None, "tile", "chan"), P(None, "chan", "tile", None)),
        check_vma=False,
    )
```

```python
import functools
import math

import jax
import jax.numpy as jnp
from jax import lax
from jax.experimental import pallas as pl
from jax.experimental.pallas import tpu as pltpu
from jax.sharding import PartitionSpec as P

DEPTHS = 256
BINS = 288
THRESHOLD = 0.8
STEP_SIZE = 0.5
MESH = pl.DeviceIdType.MESH
LANES = 128
F32 = jnp.float32
BF16 = jnp.bfloat16


def round_up(value, unit):
    return (value + unit - 1) // unit * unit


def split(x):
    high = x.astype(BF16)
    return high, (x - high.astype(F32)).astype(BF16)


def shrink_pair(a, b):
    squared = a * a + b * b
    factor = jnp.maximum(1.0 - THRESHOLD * lax.rsqrt(jnp.maximum(squared, 1e-30)), 0.0)
    return a * factor, b * factor


def aligned(row):
    return row if isinstance(row, int) else pl.multiple_of(row, 8)


def mxu(a, b):
    return jnp.dot(a, b, preferred_element_type=F32)


def kernel(
    d,
    dirty_hbm,
    beams_hbm,
    bins_hbm,
    order_hbm,
    out,
    res,
    dirty,
    beams,
    bins,
    order,
    bincol,
    at3,
    a3,
    at2,
    x,
    big,
    first_hi,
    first_lo,
    first_slots,
    model,
    padded,
    slots,
    mixed,
    send_a,
    send_d,
    send_m,
    send_r,
    recv_a,
    recv_d,
    recv_m,
    recv_h,
    recv_r,
    sems_a,
    sems_d,
    sems_m,
    sems_h,
    sems_r,
    sems_in,
):
    G, T, R, Y, C, S, W, CC, NCH, HALF, BEAM = (
        d["G"], d["T"], d["R"], d["Y"], d["C"], d["S"], d["W"], d["CC"], d["NCH"], d["HALF"], d["BEAM"]
    )
    SC = S * C
    KP = d["KP"]
    g = lax.axis_index("chan")
    t = lax.axis_index("tile")
    has_prev = t > 0
    has_next = t < T - 1
    before = lax.rem(t + T - 1, T)
    after = lax.rem(t + 1, T)

    pairs = ((dirty_hbm, dirty), (bins_hbm, bins), (beams_hbm, beams), (order_hbm, order))
    loads = [pltpu.make_async_copy(src, dst, sems_in.at[n]) for n, (src, dst) in enumerate(pairs)]
    for load in loads:
        load.start()
    barrier = pltpu.get_barrier_semaphore()
    for step in range(1, G):
        pl.semaphore_signal(barrier, inc=1, device_id=(lax.rem(g + step, G), t), device_id_type=MESH)

    @pl.when(has_prev)
    def _():
        for p in range(G):
            pl.semaphore_signal(barrier, inc=1, device_id=(p, before), device_id_type=MESH)

    @pl.when(has_next)
    def _():
        for p in range(G):
            pl.semaphore_signal(barrier, inc=1, device_id=(p, after), device_id_type=MESH)

    def pack(send, k, cells):
        for p in range(G):
            for r in range(R):
                send[p, k, r * W : r * W + W, :] = cells[pl.ds(k * W * Y + p * R + r, W, stride=Y), :]

    loads[0].wait()
    for c in range(C):
        for s in range(S):
            mixed[(c * S + s) * Y : (c * S + s) * Y + Y, :] = dirty[(s * C + c) * Y : (s * C + c) * Y + Y, :]
    for k in range(NCH):
        pack(send_a, k, mixed)
    near = has_prev.astype(jnp.int32) + has_next.astype(jnp.int32)
    pl.semaphore_wait(barrier, G - 1 + G * near)

    def own_copies(src, dst, sems, *k):
        out_copies, in_copies = [], []
        for step in range(1, G):
            p = lax.rem(g + step, G)
            out_copies.append(
                pltpu.make_async_remote_copy(
                    src(p), dst(g), sems.at[(0, p, *k)], sems.at[(1, g, *k)], device_id=(p, t), device_id_type=MESH
                )
            )
            in_copies.append(
                pltpu.make_async_remote_copy(
                    src(p), dst(p), sems.at[(0, p, *k)], sems.at[(1, p, *k)], device_id=(p, t), device_id_type=MESH
                )
            )
        return out_copies, in_copies

    out_a, in_a = own_copies(lambda p: send_a.at[p], lambda p: recv_a.at[p], sems_a)
    for copy in out_a:
        copy.start()
    recv_a[g] = send_a[g]

    for load in loads[1:]:
        load.wait()
    bincol[...] = jnp.zeros_like(bincol)
    for row in range(G * C):
        bincol[S * row : S * row + S, :] = jnp.full((S, LANES), bins[row].astype(F32))
    scale = 1.0 / math.sqrt(G * C)
    at3[...] = jnp.zeros_like(at3)
    for piece in range(DEPTHS // LANES):
        shape = (KP, LANES)
        depth = lax.broadcasted_iota(jnp.int32, shape, 1) + (piece * LANES - DEPTHS // 2)
        product = bincol[...] * depth.astype(F32)
        turns = product - BINS * jnp.floor(product * (1.0 / BINS))
        turns = jnp.where(turns < 0, turns + BINS, turns)
        turns = jnp.where(turns >= BINS, turns - BINS, turns)
        angles = turns * (2.0 * math.pi / BINS)
        row = lax.broadcasted_iota(jnp.int32, shape, 0)
        is_q = (row & 1) == 0
        real = row < G * SC
        cosine = jnp.where(real, jnp.cos(angles) * scale, 0.0)
        sine = jnp.where(real, jnp.sin(angles) * scale, 0.0)
        for half, value in ((0, jnp.where(is_q, cosine, sine)), (1, jnp.where(is_q, -sine, cosine))):
            lanes = pl.ds(half * DEPTHS + piece * LANES, LANES)
            high, low = split(value)
            at2[0:KP, lanes] = high
            at2[KP : 2 * KP, lanes] = low
            at3[0:KP, lanes] = high.astype(F32)
            at3[KP : 2 * KP, lanes] = low.astype(F32)
            at3[2 * KP : 3 * KP, lanes] = high.astype(F32)
    a3[...] = at3[...].T.astype(BF16)
    x[...] = jnp.zeros_like(x)

    shift = int(math.log2(LANES))

    def permute(cells):
        halves = []
        for h in range(Y // 8):
            pixel = order[8 * h : 8 * h + 8, :]
            col = pixel & (LANES - 1)
            row = lax.shift_right_logical(pixel, shift)
            acc = jnp.zeros((8, LANES), F32)
            for y in range(Y):
                taken = jnp.take_along_axis(cells(y), col, axis=1, mode="promise_in_bounds")
                acc = jnp.where(row == y, taken, acc)
            halves.append(acc)
        return jnp.concatenate(halves, axis=0)

    def gather_dirty(c, carry):
        for s in range(S):
            source = (s * C + c) * Y
            target = pl.ds(aligned((c * S + s) * Y), Y)
            slots[target, :] = permute(lambda y: jnp.broadcast_to(dirty[pl.ds(source + y, 1), :], (8, LANES)))
        return carry

    def project(recv):
        for q in range(G):
            for k in range(NCH):
                for r in range(R):
                    x[q * SC + k * W : q * SC + k * W + W, r * LANES : (r + 1) * LANES] = recv[
                        q, k, r * W : r * W + W, :
                    ]
        high, low = split(x[...])
        parts = [high, high, low]
        if d["K3"] > 3 * KP:
            parts.append(jnp.zeros((d["K3"] - 3 * KP, x.shape[1]), BF16))
        big[...] = mxu(a3[...], jnp.concatenate(parts, axis=0))

    BLOCK = 16

    for copy in in_a:
        copy.wait_recv()
    project(recv_a)

    def shrink_first(i, carry):
        top = pl.ds(pl.multiple_of(i * BLOCK, BLOCK), BLOCK)
        low = pl.ds(pl.multiple_of(DEPTHS + i * BLOCK, BLOCK), BLOCK)
        a, b = shrink_pair(big[top, :], big[low, :])
        first_hi[top, :], first_lo[top, :] = split(a)
        first_hi[low, :], first_lo[low, :] = split(b)
        return carry

    lax.fori_loop(0, DEPTHS // BLOCK, shrink_first, 0)
    both = mxu(at2[...], first_hi[...])
    model[...] = both[:KP] + both[KP:] + mxu(at2[0:KP, :], first_lo[...])

    up = g * R < HALF
    goes = jnp.logical_or(jnp.logical_and(up, has_prev), jnp.logical_and(jnp.logical_not(up), has_next))
    toward = jnp.where(up, before, after)
    copies_m, copies_h = [], []
    for k in range(NCH):
        for p in range(G):
            for r in range(R):
                send_m[p, k, r * W : r * W + W, :] = model[
                    p * SC + k * W : p * SC + k * W + W, r * LANES : (r + 1) * LANES
                ]
        halo = [
            pltpu.make_async_remote_copy(
                send_m.at[p, k],
                recv_h.at[g, k],
                sems_h.at[0, p, k],
                sems_h.at[1, g, k],
                device_id=(p, toward),
                device_id_type=MESH,
            )
            for p in range(G)
        ]
        copies_h.append(halo)

        @pl.when(goes)
        def _():
            for copy in halo:
                copy.start()

        copies = own_copies(
            lambda p: send_m.at[p, k], lambda p: recv_m.at[p, k], sems_m, k
        )
        copies_m.append(copies)
        for copy in copies[0]:
            copy.start()
        recv_m[g, k] = send_m[g, k]

    lax.fori_loop(0, C, gather_dirty, 0)
    for k in range(NCH):
        pack(send_d, k, slots)
    out_d, in_d = own_copies(lambda p: send_d.at[p], lambda p: recv_d.at[p], sems_d)
    for copy in out_d:
        copy.start()
    recv_d[g] = send_d[g]

    PY = Y + 2 * HALF
    lane = lax.broadcasted_iota(jnp.int32, (Y, LANES), 1)
    blocks = [range(0, (BEAM + 1) // 2), range((BEAM + 1) // 2, BEAM)]

    def convolve(c, carry):
        totals = [jnp.zeros((Y, LANES), F32) for _ in range(S)]
        for block in blocks:
            sums = [[None] * len(block) for _ in range(S)]
            for i in range(BEAM):
                rows = [padded[pl.ds((c * S + s) * PY + i, Y), :] for s in range(S)]
                for n, j in enumerate(block):
                    tap = beams[c, i * BEAM + j]
                    for s in range(S):
                        term = tap * rows[s]
                        sums[s][n] = term if i == 0 else sums[s][n] + term
            for n, j in enumerate(block):
                inside = jnp.logical_and(lane + (j - HALF) >= 0, lane + (j - HALF) < LANES)
                for s in range(S):
                    moved = sums[s][n]
                    if j != HALF:
                        moved = pltpu.roll(moved, (HALF - j) % LANES, axis=1)
                        moved = jnp.where(inside, moved, 0.0)
                    totals[s] = totals[s] + moved
        for s in range(S):
            cells = pl.ds(aligned((s * C + c) * Y), Y)
            res[cells, :] = dirty[cells, :] - totals[s]
        return carry

    def gather_res(c, carry):
        for s in range(S):
            source = (s * C + c) * Y
            target = pl.ds(aligned((c * S + s) * Y), Y)
            slots[target, :] = permute(lambda y: jnp.broadcast_to(res[pl.ds(source + y, 1), :], (8, LANES)))
        return carry

    def halo_block(q, k, ok):
        arrived = pltpu.make_async_remote_copy(
            send_m.at[q, k],
            recv_h.at[q, k],
            sems_h.at[0, q, k],
            sems_h.at[1, q, k],
            device_id=(q, t),
            device_id_type=MESH,
        )

        @pl.when(ok)
        def _():
            arrived.wait_recv()

        @pl.when(jnp.logical_not(ok))
        def _():
            recv_h[q, k] = jnp.zeros(recv_h.shape[2:], F32)

    copies_r = []

    def step(c, carry):
        gather_res(c - 1, 0)
        return convolve(c, carry)

    def send_slots(k):
        pack(send_r, k, slots)
        copies = own_copies(lambda p: send_r.at[p, k], lambda p: recv_r.at[p, k], sems_r, k)
        copies_r.append(copies)
        for copy in copies[0]:
            copy.start()
        recv_r[g, k] = send_r[g, k]

    for k in range(NCH):
        for copy in copies_m[k][1]:
            copy.wait_recv()
        for q in range(G):
            from_next = q * R < HALF
            halo_block(q, k, has_next if from_next else has_prev)
            at_row = Y + HALF + q * R if from_next else q * R - HALF
            for r in range(R):
                padded[pl.ds(k * W * PY + HALF + q * R + r, W, stride=PY), :] = recv_m[
                    q, k, r * W : r * W + W, :
                ]
                padded[pl.ds(k * W * PY + at_row + r, W, stride=PY), :] = recv_h[
                    q, k, r * W : r * W + W, :
                ]
        if k == 0:
            convolve(0, 0)
        else:
            step(k * CC, 0)
            send_slots(k - 1)
        lax.fori_loop(k * CC + 1, (k + 1) * CC, step, 0)
    gather_res(C - 1, 0)
    send_slots(NCH - 1)

    for copy in in_d:
        copy.wait_recv()
    project(recv_d)

    def shrink_slots(i, carry):
        top = pl.ds(pl.multiple_of(i * BLOCK, BLOCK), BLOCK)
        low = pl.ds(pl.multiple_of(DEPTHS + i * BLOCK, BLOCK), BLOCK)
        first_slots[top, :], first_slots[low, :] = shrink_pair(big[top, :], big[low, :])
        return carry

    lax.fori_loop(0, DEPTHS // BLOCK, shrink_slots, 0)

    for k in range(NCH):
        for copy in copies_r[k][1]:
            copy.wait_recv()
    project(recv_r)

    def finish(i, carry, tail=0):
        top = pl.ds(pl.multiple_of(i * BLOCK, BLOCK), BLOCK)
        low = pl.ds(pl.multiple_of(DEPTHS + i * BLOCK, BLOCK), BLOCK)
        a, b = shrink_pair(
            first_slots[top, :] + STEP_SIZE * big[top, :], first_slots[low, :] + STEP_SIZE * big[low, :]
        )
        for start, value in ((0, a), (DEPTHS, b)):
            for r in range(R):
                piece = value[:, r * LANES : (r + 1) * LANES]
                base = (start + i * BLOCK) * R + r
                out[pl.ds(base, BLOCK - tail, stride=R), :] = piece[: BLOCK - tail]
                if tail:
                    out[pl.ds(base + (BLOCK - tail) * R, tail), :] = piece[BLOCK - tail :]
        return carry

    lax.fori_loop(0, DEPTHS // BLOCK - 1, finish, 0)
    finish(DEPTHS // BLOCK - 1, 0, 1)

    for copy in out_a + out_d:
        copy.wait_send()
    for k in range(NCH):
        for copy in copies_m[k][0] + copies_r[k][0]:
            copy.wait_send()

    @pl.when(goes)
    def _():
        for halo in copies_h:
            for copy in halo:
                copy.wait_send()


def on_device(dirty, beams, chan_bins, pixel_order):
    S, C, Y, X = dirty.shape
    G = lax.axis_size("chan")
    T = lax.axis_size("tile")
    BEAM = math.isqrt(beams.shape[1])
    HALF = (BEAM - 1) // 2
    R = Y // G
    CC = 3 if C % 3 == 0 else C
    NCH = C // CC
    W = S * CC
    SC = S * C
    KP = round_up(G * SC, 16)
    K3 = round_up(3 * KP, LANES)
    PB = round_up(R * W, 8)
    N = R * X
    d = dict(G=G, T=T, R=R, Y=Y, C=C, S=S, W=W, CC=CC, NCH=NCH, HALF=HALF, BEAM=BEAM, KP=KP, K3=K3)
    vmem = pl.BlockSpec(memory_space=pltpu.VMEM)
    hbm = pl.BlockSpec(memory_space=pltpu.HBM)
    block = pltpu.VMEM((G, NCH, PB, LANES), F32)
    dma = pltpu.SemaphoreType.DMA
    args = (dirty.reshape(SC * Y, X), beams, chan_bins, pixel_order.reshape(Y, X))
    spectrum, residual = pl.pallas_call(
        functools.partial(kernel, d),
        out_shape=(
            jax.ShapeDtypeStruct((2 * DEPTHS * R, LANES), F32),
            jax.ShapeDtypeStruct((SC * Y, X), F32),
        ),
        in_specs=[hbm, hbm, hbm, hbm],
        out_specs=(vmem, vmem),
        scratch_shapes=[
            pltpu.VMEM((SC * Y, X), F32),
            pltpu.SMEM(beams.shape, F32),
            pltpu.SMEM(chan_bins.shape, jnp.int32),
            pltpu.VMEM((Y, X), jnp.int32),
            pltpu.VMEM((KP, LANES), F32),
            pltpu.VMEM((K3, 2 * DEPTHS), F32),
            pltpu.VMEM((2 * DEPTHS, K3), BF16),
            pltpu.VMEM((2 * KP, 2 * DEPTHS), BF16),
            pltpu.VMEM((KP, N), F32),
            pltpu.VMEM((2 * DEPTHS, N), F32),
            pltpu.VMEM((2 * DEPTHS, N), BF16),
            pltpu.VMEM((2 * DEPTHS, N), BF16),
            pltpu.VMEM((2 * DEPTHS, N), F32),
            pltpu.VMEM((KP, N), F32),
            pltpu.VMEM(((SC + 1) * (Y + 2 * HALF), LANES), F32),
            pltpu.VMEM(((SC + 1) * Y, LANES), F32),
            pltpu.VMEM(((SC + 1) * Y, LANES), F32),
        ]
        + [block] * 9
        + [dma((2, G)), dma((2, G)), dma((2, G, NCH)), dma((2, G, NCH)), dma((2, G, NCH)), dma((4,))],
        compiler_params=pltpu.CompilerParams(
            collective_id=0, has_side_effects=True, vmem_limit_bytes=48 * 1024 * 1024
        ),
    )(*(pltpu.with_memory_space_constraint(arg, pltpu.HBM) for arg in args))
    return spectrum.reshape(2, DEPTHS, 1, N), residual.reshape(dirty.shape)


def solution(mesh):
    placed = (P(None, "chan", "tile", None), P("chan", None), P(), P("tile", None))
    return jax.shard_map(
        on_device,
        mesh=mesh,
        in_specs=placed,
        out_specs=(P(None, None, "tile", "chan"), P(None, "chan", "tile", None)),
        check_vma=False,
    )
```
